1024 devices in a mesh: section: 32 (over x_hi, z), dp: 32 (over x_lo, y, core).
Axes of the slice: x: 8 (x_hi: 4, x_lo: 2; x = x_hi * 2 + x_lo), y: 8, z: 8, core: 2. Of those that a mesh axis runs over, the one named last changes fastest.
Arguments:
- queries: bfloat16 [32, 12288, 1024], P('section', 'dp'), may hold values from -600 to 600
- images: bfloat16 [32, 128, 8192], P('dp', 'section'), may hold values from -6 to 6
- w_key: bfloat16 [32, 8192, 128], P('section', 'dp'), may hold values from -0.0625 to 0.0625
- w_value: bfloat16 [32, 8192, 128], P('section', 'dp'), may hold values from -0.0625 to 0.0625
- key_gain: float32 [8, 128], replicated, may hold values from 0.1 to 1.9
- d_out: bfloat16 [32, 12288, 1024], P('section', 'dp'), may hold values from -6 to 6
- img_len: int32 [32], P('dp'), may hold values from 32 to 128, as said below
- text_start: int32 [32], P('dp'), may hold values from 0 to 191
Outputs:
- attended: bfloat16 [32, 12288, 1024], P('section', 'dp')
- d_images: float32 [32, 128, 8192], P('dp', 'section')
The draws below stay inside these ranges and needn't reach their ends.
Inputs may be any that keep to these rules, and one draw needn't show every extreme that they name: `img_len`: each sample uses a whole number of tiles of 32 tokens, 1 to 4 tiles; some sample uses all 4.
All inputs are finite; a program needn't handle non-finite values.
Results may differ from the reference program's by a relative error of at most 0.025.
Values may be sent and summed in bfloat16 or wider, within the bound.
No kernel may reach another device: no remote copies, remote signals or barrier semaphores. Data moves between devices by JAX's collectives and lax.ppermute only.
A program may use at most 32 MiB of HBM per device.

```python
import math
import jax
import jax.numpy as jnp
from jax import lax

D = 8192
HEAD = 128
KVH = 4
IMG_TOK = 128
TXT_DEV = 384
LAYERS = 8
LAYER_HEADS = 32
GROUPS = 32
TEXT = 12288
QW = 1024


def draw_queries(key, part):
    base = jnp.clip(jax.random.normal(key, (LAYER_HEADS, TEXT, QW), jnp.float32), -5.0, 5.0)
    return base.astype(jnp.bfloat16)


def draw_d_out(key, part):
    base = jnp.clip(jax.random.normal(jax.random.fold_in(key, 11), (LAYER_HEADS, TEXT, QW), jnp.float32), -6.0, 6.0)
    return base.astype(jnp.bfloat16)


def draw_img_len(key, part):
    tiles = jax.random.randint(key, (GROUPS,), 1, 5)
    chosen = jax.random.randint(jax.random.fold_in(key, 3), (), 0, GROUPS)
    tiles = jnp.where(jnp.arange(GROUPS) == chosen, 4, tiles)
    return (tiles * (IMG_TOK // 4)).astype(jnp.int32)


def plant(drawn, key, least, high):
    extent = drawn.shape
    index_at = [jax.random.randint(jax.random.fold_in(key, axis), (), 0, extent[axis]) for axis in range(len(extent))]
    drawn = drawn.at[tuple(index_at)].set(least)
    longest = extent.index(max(extent))
    index_at[longest] = (index_at[longest] + 1) % extent[longest]
    return drawn.at[tuple(index_at)].set(high)


def shard_levels(stream_key, shape, shards, least, largest):
    def one(axis_at, shards_of):
        draws = jax.random.uniform(jax.random.fold_in(jax.random.fold_in(stream_key, 6), axis_at), (shards_of,), jnp.float32, least / len(shards), largest / len(shards))
        return jnp.repeat(jnp.exp(draws), shape[axis_at] // shards_of).reshape((-1,) + (1,) * (len(shape) - axis_at - 1))

    level = one(*shards[0])
    for cut in shards[1:]:
        level = level * one(*cut)
    return level


def normal_values(rng, shape, scale, reach, pieces=(), dtype=jnp.bfloat16):
    values = scale * jax.random.normal(rng, shape, jnp.float32)
    if pieces:
        values = values * shard_levels(rng, shape, pieces, -0.22, 0.18)
    return jnp.clip(values, -reach, reach).astype(dtype)


def setup_inputs(seed: int = 0) -> dict:
    key_list = jax.random.split(jax.random.key(seed), 9)
    return {
        "queries": draw_queries(jax.random.fold_in(key_list[8], 71), 0),
        "images": normal_values(key_list[1], (GROUPS, IMG_TOK, D), 1.0, 6.0, ((0, 32), (1, 32))),
        "w_key": normal_values(key_list[2], (LAYER_HEADS, D, HEAD), D ** -0.5, 0.0625, ((0, 32), (1, 32))),
        "w_value": normal_values(key_list[3], (LAYER_HEADS, D, HEAD), D ** -0.5, 0.0625, ((0, 32), (1, 32))),
        "key_gain": jnp.clip(1.0 + 0.18 * jax.random.normal(key_list[4], (LAYERS, HEAD), jnp.float32), 0.1, 1.9),
        "d_out": draw_d_out(jax.random.fold_in(key_list[8], 71), 0),
        "img_len": draw_img_len(jax.random.fold_in(key_list[8], 71), 0),
        "text_start": plant(jax.random.randint(key_list[7], (GROUPS,), 0, TXT_DEV // 2), jax.random.fold_in(key_list[7], 1), 0, (TXT_DEV // 2) - 1).astype(jnp.int32),
    }


def attend(key_raw, value_raw, key_gain, queries, length, start):
    inverse = lax.rsqrt(lax.optimization_barrier(jnp.mean(key_raw * key_raw, axis=-1, keepdims=True)) + 1e-05)
    keys = (key_raw * inverse * key_gain).astype(jnp.bfloat16)
    values = value_raw.astype(jnp.bfloat16)
    head_size = key_gain.shape[-1]
    heads = queries.reshape(queries.shape[0], -1, head_size).astype(jnp.float32)
    scores = jnp.einsum('thd,jd->htj', heads, keys.astype(jnp.float32)) / math.sqrt(head_size)
    usable = jnp.arange(keys.shape[0]) < length
    scores = jnp.where(usable, scores, -1e+30)
    scores = scores - lax.optimization_barrier(jnp.max(scores, axis=-1, keepdims=True))
    expo = jnp.exp(scores)
    probs = (expo / lax.optimization_barrier(jnp.sum(expo, axis=-1, keepdims=True))).astype(jnp.bfloat16)
    mixed = jnp.einsum('htj,jd->thd', probs.astype(jnp.float32), values.astype(jnp.float32))
    mixed = mixed.reshape(queries.shape[0], -1)
    shown = jnp.arange(queries.shape[0]) >= start
    return jnp.where(shown[:, None], mixed, 0.0)

def one_sample(image_rows, key_weight, value_weight, gain, query_rows, cotangent, length, start):
    key_raw = jnp.dot(image_rows, key_weight, preferred_element_type=jnp.float32)
    value_raw = jnp.dot(image_rows, value_weight, preferred_element_type=jnp.float32)
    mixed, pull_back = jax.vjp(lambda kr, vr: attend(kr, vr, gain, query_rows, length, start), key_raw, value_raw)
    d_key, d_value = pull_back(cotangent.astype(jnp.float32))
    term = jnp.dot(d_key.astype(jnp.bfloat16), key_weight.T, preferred_element_type=jnp.float32)
    term = term + jnp.dot(d_value.astype(jnp.bfloat16), value_weight.T, preferred_element_type=jnp.float32)
    rounded = lax.optimization_barrier(term.astype(jnp.bfloat16))
    return (mixed.astype(jnp.bfloat16), rounded.astype(jnp.float32))

def reference(queries, images, w_key, w_value, key_gain, d_out, img_len, text_start):
    query_blocks = queries.reshape(LAYER_HEADS, GROUPS, TXT_DEV, QW)
    grad_blocks = d_out.reshape(LAYER_HEADS, GROUPS, TXT_DEV, QW)
    gains = jnp.repeat(key_gain, KVH, axis=0)

    def per_head(total, items):
        query_section, grad_section, key_weight, value_weight, gain = items
        mixed, terms = jax.vmap(lambda rows, qrows, grows, length, start: one_sample(rows, key_weight, value_weight, gain, qrows, grows, length, start))(images, query_section, grad_section, img_len, text_start)
        return (total + terms, mixed)
    start_total = jnp.zeros((GROUPS, IMG_TOK, D), jnp.float32)
    total, outputs = lax.scan(per_head, start_total, (query_blocks, grad_blocks, w_key, w_value, gains))
    return (outputs.reshape(LAYER_HEADS, TEXT, QW), total)
```

```python
import math

import jax
import jax.numpy as jnp
from jax import lax
from jax.sharding import Mesh
from jax.sharding import PartitionSpec as P

KVH = 4
PAIR = 2
SECTION = ("rest", "pair")
DP = ("xl", "y", "c")


def attend(key_raw, value_raw, key_gain, queries, length, start):
    inverse = lax.rsqrt(jnp.mean(key_raw * key_raw, axis=-1, keepdims=True) + 1e-05)
    keys = (key_raw * inverse * key_gain).astype(jnp.bfloat16)
    values = value_raw.astype(jnp.bfloat16)
    head_size = key_gain.shape[-1]
    heads = queries.reshape(queries.shape[0], -1, head_size).astype(jnp.float32)
    scores = jnp.einsum("thd,jd->htj", heads, keys.astype(jnp.float32)) / math.sqrt(head_size)
    usable = jnp.arange(keys.shape[0]) < length
    scores = jnp.where(usable, scores, -1e30)
    scores = scores - jnp.max(scores, axis=-1, keepdims=True)
    expo = jnp.exp(scores)
    probs = (expo / jnp.sum(expo, axis=-1, keepdims=True)).astype(jnp.bfloat16)
    mixed = jnp.einsum("htj,jd->thd", probs.astype(jnp.float32), values.astype(jnp.float32))
    mixed = mixed.reshape(queries.shape[0], -1)
    shown = jnp.arange(queries.shape[0]) >= start
    return jnp.where(shown[:, None], mixed, 0.0)


def local(queries, images, w_key, w_value, key_gain, d_out, img_len, text_start):
    rows, model = images.shape[1:]
    ny = lax.axis_size("y")
    nrest = lax.axis_size("rest")
    head = w_key.shape[-1]
    unit = w_key.shape[1] // PAIR
    nxc = lax.axis_size("xl") * lax.axis_size("c")
    own = jnp.concatenate([w_key[0], w_value[0]], axis=1).reshape(PAIR, 1, unit, 2 * head)
    own = jnp.broadcast_to(own, (PAIR, nxc, unit, 2 * head)).reshape(PAIR * nxc, unit, 2 * head)
    near = lax.all_to_all(own, ("pair", "xl", "c"), 0, 0)
    weight = lax.all_gather(near, "y", axis=0, tiled=True)
    weight = weight.reshape(ny, PAIR, nxc * unit, 2 * head)

    pieces = images[0].reshape(rows, 2, ny, 2, PAIR, unit).transpose(4, 2, 1, 3, 0, 5)
    pieces = pieces.reshape(PAIR, ny * nxc, rows, unit)
    halves = lax.all_to_all(pieces, "pair", 0, 0)
    mine = halves.transpose(1, 0, 2, 3).reshape(ny * nxc, PAIR * rows, unit)
    spread = jnp.broadcast_to(mine[None], (nrest,) + mine.shape)
    full = lax.all_to_all(spread, "rest", 0, 0)
    tokens = nrest * PAIR * rows
    image_half = full.transpose(0, 2, 1, 3).reshape(tokens, ny, nxc * unit)

    part = jnp.einsum("tyr,yhrn->htn", image_half, weight, preferred_element_type=jnp.float32)
    both = lax.all_to_all(part, "pair", 0, 0)
    raw = both[0] + both[1]

    layer = lax.axis_index(SECTION) // KVH
    gain = lax.dynamic_index_in_dim(key_gain, layer, 0, keepdims=False)
    mixed, pull_back = jax.vjp(
        lambda kr, vr: attend(kr, vr, gain, queries[0], img_len[0], text_start[0]),
        raw[:, :head],
        raw[:, head:],
    )
    d_key, d_value = pull_back(d_out[0].astype(jnp.float32))
    d_own = jnp.concatenate([d_key, d_value], axis=1).astype(jnp.bfloat16)
    d_both = lax.all_gather(d_own, "pair", axis=0)
    term = jnp.einsum("htn,yhrn->tyr", d_both, weight, preferred_element_type=jnp.float32)
    term = term.astype(jnp.bfloat16).reshape(nrest, PAIR * rows, model // PAIR)
    terms = lax.all_to_all(term, "rest", 0, 0)
    total = jnp.sum(terms.astype(jnp.float32), axis=0)
    total = total.reshape(PAIR, rows, model // PAIR)
    grads = lax.all_to_all(total, "pair", 0, 0)
    grads = grads.reshape(PAIR, rows, ny, 2, 2, unit).transpose(1, 3, 2, 4, 0, 5)
    return mixed.astype(jnp.bfloat16)[None], grads.reshape(1, rows, model)


def solution(mesh):
    sections, samples = mesh.shape["section"], mesh.shape["dp"]
    fine = Mesh(
        mesh.devices.reshape(sections // PAIR, PAIR, 2, samples // 4, 2), SECTION + DP
    )
    return jax.shard_map(
        local,
        mesh=fine,
        in_specs=(
            P(SECTION, DP, None),
            P(DP, SECTION, None),
            P(SECTION, DP, None),
            P(SECTION, DP, None),
            P(),
            P(SECTION, DP, None),
            P(DP),
            P(DP),
        ),
        out_specs=(P(SECTION, DP, None), P(DP, SECTION, None)),
        check_vma=False,
    )
```

```python
import math

import jax
import jax.numpy as jnp
from jax import lax
from jax.sharding import Mesh
from jax.sharding import PartitionSpec as P


KVH = 4
QUAD = 4
REST = ("xh", "zh")
SECTION = REST + ("quad",)
DP = ("xl", "y", "c")


def attend(key_raw, value_raw, key_gain, queries, usable, start):
    inverse = lax.rsqrt(jnp.mean(key_raw * key_raw, axis=-1, keepdims=True) + 1e-05)
    keys = (key_raw * inverse * key_gain).astype(jnp.bfloat16)
    values = value_raw.astype(jnp.bfloat16)
    head_size = key_gain.shape[-1]
    heads = queries.reshape(queries.shape[0], -1, head_size).astype(jnp.float32)
    scores = jnp.einsum("thd,jd->htj", heads, keys.astype(jnp.float32)) / math.sqrt(head_size)
    scores = jnp.where(usable, scores, -1e30)
    scores = scores - jnp.max(scores, axis=-1, keepdims=True)
    expo = jnp.exp(scores)
    probs = (expo / jnp.sum(expo, axis=-1, keepdims=True)).astype(jnp.bfloat16)
    mixed = jnp.einsum("htj,jd->thd", probs.astype(jnp.float32), values.astype(jnp.float32))
    mixed = mixed.reshape(queries.shape[0], -1)
    shown = jnp.arange(queries.shape[0]) >= start
    return jnp.where(shown[:, None], mixed, 0.0)


def local(queries, images, w_key, w_value, key_gain, d_out, img_len, text_start):
    rows, model = images.shape[1:]
    ny, nrest = lax.axis_size("y"), lax.axis_size(REST)
    head = w_key.shape[-1]
    unit = w_key.shape[1] // QUAD
    wide = 2 * unit

    own = jnp.concatenate([w_key[0], w_value[0]], axis=1).reshape(QUAD, 1, unit, 2 * head)
    own = jnp.broadcast_to(own, (QUAD, 2, unit, 2 * head)).reshape(QUAD * 2, unit, 2 * head)
    near = lax.all_to_all(own, ("quad", "xl"), 0, 0)
    weight = lax.all_to_all(jnp.broadcast_to(near[None], (ny,) + near.shape), "y", 0, 0)
    weight = weight.reshape(ny, QUAD, wide, 2 * head)

    core = lax.axis_index("c")
    pieces = images[0].reshape(rows, 2, ny, 2, QUAD, unit).transpose(3, 4, 2, 0, 1, 5)
    pieces = pieces.reshape(2, QUAD, ny, rows, wide)
    pieces = lax.all_gather(pieces, "c", axis=0)
    pieces = lax.dynamic_index_in_dim(pieces, core, 1, keepdims=False)
    pieces = lax.all_gather(pieces, "quad", axis=0)
    pieces = lax.dynamic_index_in_dim(pieces, lax.axis_index("quad"), 2, keepdims=False)
    pieces = pieces.transpose(1, 2, 0, 3, 4).reshape(2, ny, QUAD * rows, wide)
    pieces = lax.all_gather(pieces, "zh", axis=0)
    image = lax.all_gather(pieces, "xh", axis=0)
    image = image.reshape((nrest,) + image.shape[2:])

    theirs = lax.dynamic_index_in_dim(image, 1 - core, 1, keepdims=False)
    part = jnp.einsum("zyrd,yhdn->hzrn", theirs, weight, preferred_element_type=jnp.float32)
    part = lax.ppermute(part, "c", [(0, 1), (1, 0)])
    mine = lax.dynamic_index_in_dim(image, core, 1, keepdims=False)
    part = part + jnp.einsum("zyrd,yhdn->hzrn", mine, weight, preferred_element_type=jnp.float32)
    part = part.reshape(QUAD, nrest * QUAD * rows, 2 * head)
    coarse = lax.reduce_precision(part[:, :, :head], 8, 7)
    part = jnp.concatenate([coarse, part[:, :, :head] - coarse, part[:, :, head:]], axis=2)
    part = lax.all_to_all(part.astype(jnp.bfloat16), "quad", 0, 0)
    part = jnp.sum(part.astype(jnp.float32), axis=0)
    key_raw = part[:, :head] + part[:, head : 2 * head]
    value_raw = part[:, 2 * head :]

    layer = lax.axis_index(SECTION) // KVH
    usable = jnp.arange(nrest * QUAD * rows) < img_len[0]
    gain = lax.dynamic_index_in_dim(key_gain, layer, 0, keepdims=False)
    mixed, pull_back = jax.vjp(
        lambda kr, vr: attend(kr, vr, gain, queries[0], usable, text_start[0]),
        key_raw,
        value_raw,
    )
    d_key, d_value = pull_back(d_out[0].astype(jnp.float32))
    d_own = jnp.concatenate([d_key, d_value], axis=1).astype(jnp.bfloat16)
    d_heads = lax.all_to_all(jnp.broadcast_to(d_own[None], (QUAD,) + d_own.shape), "quad", 0, 0)
    d_both = lax.all_gather(d_heads, "c", axis=0)

    d_both = d_both.reshape(2, QUAD, nrest, QUAD * rows, 2 * head)
    term = jnp.einsum("shzrn,yhdn->zsyrd", d_both, weight, preferred_element_type=jnp.float32)
    term = lax.all_to_all(term.astype(jnp.bfloat16), REST, 0, 0)
    total = jnp.sum(term.astype(jnp.float32), axis=0)
    total = total.reshape(2, ny, QUAD, rows, wide).transpose(2, 0, 1, 3, 4)
    total = total.reshape(QUAD * 2, ny, rows, wide)
    grads = lax.all_to_all(total, ("quad", "c"), 0, 0)
    grads = grads.reshape(QUAD, 2, ny, rows, 2, unit).transpose(3, 4, 2, 1, 0, 5)
    return mixed.astype(jnp.bfloat16)[None], grads.reshape(1, rows, model)


def solution(mesh):
    sections, samples = mesh.shape["section"], mesh.shape["dp"]
    fine = Mesh(mesh.devices.reshape(sections // (2 * QUAD), 2, QUAD, 2, samples // 4, 2), SECTION + DP)
    return jax.shard_map(
        local,
        mesh=fine,
        in_specs=(
            P(SECTION, DP, None),
            P(DP, SECTION, None),
            P(SECTION, DP, None),
            P(SECTION, DP, None),
            P(),
            P(SECTION, DP, None),
            P(DP),
            P(DP),
        ),
        out_specs=(P(SECTION, DP, None), P(DP, SECTION, None)),
        check_vma=False,
    )
```

```python
import math

import jax
import jax.numpy as jnp
from jax import lax
from jax.sharding import Mesh
from jax.sharding import PartitionSpec as P


KVH = 4
QUAD = 4
REST = ("xh", "zh")
SECTION = REST + ("quad",)
DP = ("xl", "y", "c")


def attend(key_raw, value_raw, key_gain, queries, usable, start):
    inverse = lax.rsqrt(jnp.mean(key_raw * key_raw, axis=-1, keepdims=True) + 1e-05)
    keys = (key_raw * inverse * key_gain).astype(jnp.bfloat16)
    values = value_raw.astype(jnp.bfloat16)
    head_size = key_gain.shape[-1]
    heads = queries.reshape(queries.shape[0], -1, head_size).astype(jnp.float32)
    scores = jnp.einsum("thd,jd->htj", heads, keys.astype(jnp.float32)) / math.sqrt(head_size)
    scores = jnp.where(usable, scores, -1e30)
    scores = scores - jnp.max(scores, axis=-1, keepdims=True)
    expo = jnp.exp(scores)
    probs = (expo / jnp.sum(expo, axis=-1, keepdims=True)).astype(jnp.bfloat16)
    mixed = jnp.einsum("htj,jd->thd", probs.astype(jnp.float32), values.astype(jnp.float32))
    mixed = mixed.reshape(queries.shape[0], -1)
    shown = jnp.arange(queries.shape[0]) >= start
    return jnp.where(shown[:, None], mixed, 0.0)


def local(queries, images, w_key, w_value, key_gain, d_out, img_len, text_start):
    rows, model = images.shape[1:]
    ny, nrest = lax.axis_size("y"), lax.axis_size(REST)
    head = w_key.shape[-1]
    unit = w_key.shape[1] // QUAD
    wide = 2 * unit

    own = jnp.concatenate([w_key[0], w_value[0]], axis=1).reshape(QUAD, 1, unit, 2 * head)
    own = jnp.broadcast_to(own, (QUAD, 2, unit, 2 * head)).reshape(QUAD * 2, unit, 2 * head)
    near = lax.all_to_all(own, ("quad", "xl"), 0, 0)
    weight = lax.all_to_all(jnp.broadcast_to(near[None], (ny,) + near.shape), "y", 0, 0)
    weight = weight.reshape(ny, QUAD, wide, 2 * head)

    core = lax.axis_index("c")
    pieces = images[0].reshape(rows, 2, ny, 2, QUAD, unit).transpose(3, 4, 2, 0, 1, 5)
    pieces = pieces.reshape(2, QUAD, ny, rows, wide)
    pieces = lax.all_gather(pieces, "c", axis=0)
    pieces = lax.dynamic_index_in_dim(pieces, core, 1, keepdims=False)
    pieces = lax.all_gather(pieces, "quad", axis=0)
    pieces = lax.dynamic_index_in_dim(pieces, lax.axis_index("quad"), 2, keepdims=False)
    pieces = pieces.transpose(1, 2, 0, 3, 4).reshape(2, ny, QUAD * rows, wide)
    pieces = lax.all_gather(pieces, "zh", axis=0)
    image = lax.all_gather(pieces, "xh", axis=0)
    image = image.reshape((nrest,) + image.shape[2:])

    theirs = lax.dynamic_index_in_dim(image, 1 - core, 1, keepdims=False)
    part = jnp.einsum("zyrd,yhdn->hzrn", theirs, weight, preferred_element_type=jnp.float32)
    part = lax.ppermute(part, "c", [(0, 1), (1, 0)])
    mine = lax.dynamic_index_in_dim(image, core, 1, keepdims=False)
    part = part + jnp.einsum("zyrd,yhdn->hzrn", mine, weight, preferred_element_type=jnp.float32)
    part = part.reshape(QUAD, nrest * QUAD * rows, 2 * head)
    coarse = lax.reduce_precision(part[:, :, :head], 8, 7)
    part = jnp.concatenate([coarse, part[:, :, :head] - coarse, part[:, :, head:]], axis=2)
    part = lax.all_to_all(part.astype(jnp.bfloat16), "quad", 0, 0)
    part = jnp.sum(part.astype(jnp.float32), axis=0)
    key_raw = part[:, :head] + part[:, head : 2 * head]
    value_raw = part[:, 2 * head :]

    layer = lax.axis_index(SECTION) // KVH
    usable = jnp.arange(nrest * QUAD * rows) < img_len[0]
    gain = lax.dynamic_index_in_dim(key_gain, layer, 0, keepdims=False)
    mixed, pull_back = jax.vjp(
        lambda kr, vr: attend(kr, vr, gain, queries[0], usable, text_start[0]),
        key_raw,
        value_raw,
    )
    d_key, d_value = pull_back(d_out[0].astype(jnp.float32))
    d_own = jnp.concatenate([d_key, d_value], axis=1).astype(jnp.bfloat16)
    d_heads = lax.all_to_all(jnp.broadcast_to(d_own[None], (QUAD,) + d_own.shape), "quad", 0, 0)
    d_both = lax.all_gather(d_heads, "c", axis=0)

    d_both = d_both.reshape(2, QUAD, nrest, QUAD * rows, 2 * head)
    term = jnp.einsum("shzrn,yhdn->zsyrd", d_both, weight, preferred_element_type=jnp.float32)
    term = term.astype(jnp.bfloat16).reshape((nrest // 2, 2) + term.shape[1:])
    term = lax.all_to_all(term, "xh", 0, 0)
    total = jnp.sum(term.astype(jnp.float32), axis=0).astype(jnp.bfloat16)
    total = total.reshape(2, 2, ny, QUAD, rows, wide).transpose(0, 3, 1, 2, 4, 5)
    total = total.reshape(2 * QUAD * 2, ny, rows, wide)
    grads = lax.all_to_all(total, ("zh", "quad", "c"), 0, 0)
    grads = grads.reshape(2, QUAD, 2, ny, rows, wide)
    grads = grads[0].astype(jnp.float32) + grads[1].astype(jnp.float32)
    grads = grads.reshape(QUAD, 2, ny, rows, 2, unit).transpose(3, 4, 2, 1, 0, 5)
    return mixed.astype(jnp.bfloat16)[None], grads.reshape(1, rows, model)


def solution(mesh):
    sections, samples = mesh.shape["section"], mesh.shape["dp"]
    fine = Mesh(mesh.devices.reshape(sections // (2 * QUAD), 2, QUAD, 2, samples // 4, 2), SECTION + DP)
    return jax.shard_map(
        local,
        mesh=fine,
        in_specs=(
            P(SECTION, DP, None),
            P(DP, SECTION, None),
            P(SECTION, DP, None),
            P(SECTION, DP, None),
            P(),
            P(SECTION, DP, None),
            P(DP),
            P(DP),
        ),
        out_specs=(P(SECTION, DP, None), P(DP, SECTION, None)),
        check_vma=False,
    )
```
